32 devices in a mesh: row: 2 (over x), col: 8 (over z, y), rep: 2 (over core).
Axes of the slice: x: 2, y: 2, z: 4, core: 2. Of those that a mesh axis runs over, the one named last changes fastest.
Arguments:
- vectors: bfloat16 [128, 2048], P('rep', ('row', 'col')), may hold values from -6 to 6
- tile_values: bfloat16 [2304, 128, 128], P(('row', 'col')), may hold values from -6 to 6
- tile_rows: int32 [2304], P(('row', 'col')), may hold values from 0 to 7
- tile_cols: int32 [2304], P(('row', 'col')), may hold values from 0 to 1
- tile_scales: float32 [2304], P(('row', 'col')), may hold values from 0.5 to 2
- live_tiles: int32 [16], P(('row', 'col')), may hold values from 1 to 144, as said below
Outputs:
- basis: float32 [128, 2048], P('rep', ('row', 'col'))
- ritz: float32 [128, 128], replicated
The draws below stay inside these ranges and needn't reach their ends.
Inputs may be any that keep to these rules, and one draw needn't show every extreme that they name: `live_tiles`: some pair of row and col indices has all 144 of its slots filled.
All inputs are finite; a program needn't handle non-finite values.
Results may differ from the reference program's by a relative error of at most 0.03.
Values may be sent and summed in bfloat16 or wider, within the bound.
A program may use at most 64 MiB of HBM per device.

```python
import math
import jax
import jax.numpy as jnp
from jax import lax

BLOCK = 128
VECTORS = 128
LOCAL_BLOCKS = 1
TILES_DEV = 144
DEGREE = 3
ROW_BLOCKS = 8
PANEL_BLOCKS = 2
GRID = 16
TILES = 2304
ROWS = 2048
N_ROW = 2
N_COL = 8


def draw_live_tiles(key, part):
    key_base, key_heavy, key_pick = jax.random.split(key, 3)
    lowest = max(TILES_DEV // 8, 1)
    base = jax.random.randint(key_base, (GRID,), lowest, TILES_DEV // 2 + 1, dtype=jnp.int32)
    heavy = jax.random.randint(key_heavy, (GRID,), 0, 8, dtype=jnp.int32) == 0
    counts = jnp.where(heavy, jnp.int32(TILES_DEV), base)
    chosen = jax.random.randint(key_pick, (), 0, GRID, dtype=jnp.int32)
    return counts.at[chosen].set(jnp.int32(TILES_DEV))


def with_ends(values, key, least, largest):
    extent = values.shape
    place = [jax.random.randint(jax.random.fold_in(key, axis), (), 0, extent[axis]) for axis in range(len(extent))]
    values = values.at[tuple(place)].set(least)
    longest = extent.index(max(extent))
    place[longest] = (place[longest] + 1) % extent[longest]
    return values.at[tuple(place)].set(largest)


def block_levels(own_key, shape, pieces, smallest, largest):
    level = 1.0
    for axis_at, blocks in pieces:
        heights = jax.random.uniform(jax.random.fold_in(jax.random.fold_in(own_key, 6), axis_at), (blocks,), jnp.float32, smallest / len(pieces), largest / len(pieces))
        level = level * jnp.repeat(jnp.exp(heights), shape[axis_at] // blocks).reshape((-1,) + (1,) * (len(shape) - 1 - axis_at))
    return level


def noise(key, dims, width, most, pieces=(), kind=jnp.bfloat16):
    gain = block_levels(key, dims, pieces, -0.22, 0.18) if pieces else 1.0
    result = jax.random.normal(key, dims, jnp.float32) * width * gain
    return jnp.minimum(jnp.maximum(result, -most), most).astype(kind)


def setup_inputs(seed: int = 0) -> dict:
    seeds = jax.random.split(jax.random.key(seed), 7)
    return {
        "vectors": noise(seeds[0], (VECTORS, ROWS), 1.0, 6.0, ((0, 2), (1, 16))),
        "tile_values": noise(seeds[1], (TILES, BLOCK, BLOCK), 1.0, 6.0, ((0, 16),)),
        "tile_rows": with_ends(jax.random.randint(seeds[2], (TILES,), 0, ROW_BLOCKS), jax.random.fold_in(seeds[2], 1), 0, ROW_BLOCKS - 1).astype(jnp.int32),
        "tile_cols": with_ends(jax.random.randint(seeds[3], (TILES,), 0, PANEL_BLOCKS), jax.random.fold_in(seeds[3], 1), 0, PANEL_BLOCKS - 1).astype(jnp.int32),
        "tile_scales": jnp.clip(jnp.exp(math.log(2.0) - 1.3862944 * jax.random.uniform(seeds[4], (TILES,), jnp.float32) ** block_levels(seeds[4], (TILES,), ((0, 16),), -0.2, 0.2)), 0.5, 2.0),
        "live_tiles": draw_live_tiles(jax.random.fold_in(seeds[6], 71), 0),
    }


def slot_weights(rows_here, scales_here, live_here, row_blocks):
    slots = jnp.arange(rows_here.shape[0], dtype=jnp.int32)
    alive = (slots < live_here).astype(jnp.float32)
    onehot = (rows_here[None, :] == jnp.arange(row_blocks, dtype=jnp.int32)[:, None]).astype(jnp.float32)
    return onehot * (scales_here * alive)[None, :]

def reference(vectors, tile_values, tile_rows, tile_cols, tile_scales, live_tiles):
    highest = lax.Precision.HIGHEST
    count_vec = vectors.shape[0]
    grid_tiles = tile_values.reshape(GRID, TILES_DEV, BLOCK, BLOCK)
    grid_rows = tile_rows.reshape(GRID, TILES_DEV)
    grid_cols = tile_cols.reshape(GRID, TILES_DEV)
    grid_scales = tile_scales.reshape(GRID, TILES_DEV)

    def degree_group(row_group):

        def add_col(running, col_group):
            device = (row_group * N_COL + col_group).astype(jnp.int32)
            here = lax.dynamic_index_in_dim(grid_tiles, device, 0, keepdims=False)
            weights = slot_weights(lax.dynamic_index_in_dim(grid_rows, device, 0, keepdims=False), lax.dynamic_index_in_dim(grid_scales, device, 0, keepdims=False), live_tiles[device], ROW_BLOCKS)
            absolute = lax.optimization_barrier(jnp.sum(jnp.abs(here.astype(jnp.float32)), axis=2))
            return (running + jnp.dot(weights, absolute, precision=highest), None)
        running, _ = lax.scan(add_col, jnp.zeros((ROW_BLOCKS, BLOCK), jnp.float32), jnp.arange(N_COL, dtype=jnp.int32))
        return running
    degree_sums = lax.map(degree_group, jnp.arange(N_ROW, dtype=jnp.int32)).reshape(ROWS)
    inv_root = lax.rsqrt(1.0 + degree_sums)

    def apply_operator(current):
        blocks_five = current.reshape(count_vec, N_ROW, N_COL, LOCAL_BLOCKS, BLOCK)

        def row_part(row_group):

            def add_col(running, col_group):
                device = (row_group * N_COL + col_group).astype(jnp.int32)
                column_set = lax.dynamic_index_in_dim(blocks_five, col_group, 2, keepdims=False)
                column_set = column_set.reshape(count_vec, PANEL_BLOCKS, BLOCK).transpose(1, 0, 2)
                cols_here = lax.dynamic_index_in_dim(grid_cols, device, 0, keepdims=False)
                picked = column_set[cols_here]
                here = lax.dynamic_index_in_dim(grid_tiles, device, 0, keepdims=False)
                products = jnp.einsum('tkj,tij->tki', picked.astype(jnp.float32), here.astype(jnp.float32), precision=highest)
                weights = slot_weights(lax.dynamic_index_in_dim(grid_rows, device, 0, keepdims=False), lax.dynamic_index_in_dim(grid_scales, device, 0, keepdims=False), live_tiles[device], ROW_BLOCKS)
                partial_sum = jnp.dot(weights, products.reshape(TILES_DEV, count_vec * BLOCK), precision=highest)
                return (running + partial_sum.astype(jnp.bfloat16).astype(jnp.float32), None)
            running, _ = lax.scan(add_col, jnp.zeros((ROW_BLOCKS, count_vec * BLOCK), jnp.float32), jnp.arange(N_COL, dtype=jnp.int32))
            return running
        sums = lax.map(row_part, jnp.arange(N_ROW, dtype=jnp.int32))
        sums = sums.reshape(N_ROW * ROW_BLOCKS, count_vec, BLOCK).transpose(1, 0, 2).reshape(count_vec, ROWS)
        return sums * inv_root[None, :]
    previous = vectors
    current = apply_operator(previous).astype(jnp.bfloat16)
    for index in range(DEGREE - 1):
        following = (2.0 * apply_operator(current) - previous.astype(jnp.float32)).astype(jnp.bfloat16)
        previous, current = (current, following)
    image = apply_operator(current)
    filtered = current.astype(jnp.float32)
    gram = jnp.dot(filtered, filtered.T, precision=highest)
    cross = jnp.dot(filtered, image.T, precision=highest)
    lower = jnp.linalg.cholesky(gram)
    factor = math.sqrt(ROWS)
    basis = factor * jax.scipy.linalg.solve_triangular(lower, filtered, lower=True)
    left_solved = jax.scipy.linalg.solve_triangular(lower, cross, lower=True)
    ritz = factor * jax.scipy.linalg.solve_triangular(lower, left_solved.T, lower=True).T
    return (basis, ritz)
```

```python
import functools
import math

import jax
import jax.numpy as jnp
from jax import lax
from jax.experimental import pallas as pl
from jax.experimental.pallas import tpu as pltpu
from jax.sharding import PartitionSpec as P

DEGREE = 3
HIGHEST = lax.Precision.HIGHEST
MESH = pl.DeviceIdType.MESH
F32 = jnp.float32
BF16 = jnp.bfloat16


def pieces_of(count, want):
    while count % want:
        want -= 1
    return want


def assemble(
    row_blocks, panel_blocks, chunks,
    rows_ref, cols_ref, scales_ref, live_ref, rep_ref, tiles_ref,
    high_ref, low_ref, degree_ref, held, total, absolute, sems,
):
    slots, half, block = held.shape
    step = slots // chunks
    copies = []
    first = pl.multiple_of(rep_ref[0] * half, half)
    for c in range(chunks):
        part = pl.ds(c * step, step)
        copy = pltpu.make_async_copy(
            tiles_ref.at[part, pl.ds(first, half), :], held.at[part], sems.at[c]
        )
        copy.start()
        copies.append(copy)
    total[...] = jnp.zeros_like(total)
    absolute[...] = jnp.zeros_like(absolute)
    live = live_ref[0]
    for c in range(chunks):
        copies[c].wait()

        def body(t, carry):
            scale = jnp.where(t < live, scales_ref[t], 0.0)
            row = rows_ref[t]
            values = held[t].astype(F32)
            place = row * panel_blocks + cols_ref[t]
            total[place] = total[place] + values * scale
            absolute[row] = absolute[row] + jnp.abs(values) * scale
            return carry

        lax.fori_loop(c * step, (c + 1) * step, body, 0, unroll=4)
    for r in range(row_blocks):
        for c in range(panel_blocks):
            whole = total[r * panel_blocks + c]
            high = whole.astype(BF16)
            high_ref[r * half : (r + 1) * half, c * block : (c + 1) * block] = high
            low_ref[r * half : (r + 1) * half, c * block : (c + 1) * block] = (
                whole - high.astype(F32)
            ).astype(BF16)
    degree_ref[...] = jnp.zeros_like(degree_ref)
    for p in range(row_blocks // 2):
        pair = absolute[2 * p : 2 * p + 2].reshape(2 * half, block)
        degree_ref[p : p + 1, :] = jnp.sum(pair.T, axis=0, keepdims=True)


def contract(a, b, dims):
    return lax.dot_general(a, b, (dims, ((), ())), preferred_element_type=F32)


def split(value):
    high = value.astype(BF16)
    return high, (value - high.astype(F32)).astype(BF16)


def exchange(
    n_row, n_col, n_rep,
    high_ref, low_ref, degree_ref, vectors_ref,
    gram_ref, cross_ref, block_ref,
    raw, degrees, panels, sends, lands, owners, inv, grams, cross_send, cross_one, cross_two, cross_all,
    g_send, g_recv, c_send, c_recv,
):
    row, col, rep = lax.axis_index("row"), lax.axis_index("col"), lax.axis_index("rep")
    n_group = n_row * n_rep
    me = row * n_rep + rep
    half = vectors_ref.shape[0]
    count = half * n_rep

    def group_peer(k):
        other = lax.rem(me + k, n_group)
        return (lax.div(other, n_rep), col, lax.rem(other, n_rep))

    def col_peer(k):
        return (row, lax.rem(col + k, n_col), rep)

    barrier = pltpu.get_barrier_semaphore()
    for k in range(1, n_group):
        pl.semaphore_signal(barrier, inc=1, device_id=group_peer(k), device_id_type=MESH)
    for k in range(1, n_col):
        pl.semaphore_signal(barrier, inc=1, device_id=col_peer(k), device_id_type=MESH)
    pl.semaphore_wait(barrier, n_group + n_col - 2)

    started = []

    def to_group(phase, source, target):
        out = []
        for k in range(1, n_group):
            copy = pltpu.make_async_remote_copy(
                src_ref=source(lax.rem(me + k, n_group)), dst_ref=target,
                send_sem=g_send.at[phase, k - 1], recv_sem=g_recv.at[phase, k - 1],
                device_id=group_peer(k), device_id_type=MESH,
            )
            copy.start()
            out.append(copy)
        started.extend(out)
        return out

    def to_col(phase, source, target):
        out = []
        order = sorted(range(1, n_col), key=lambda k: -min(k, n_col - k))
        for k in order:
            copy = pltpu.make_async_remote_copy(
                src_ref=source(lax.rem(col + k, n_col)), dst_ref=target,
                send_sem=c_send.at[phase, k - 1], recv_sem=c_recv.at[phase, k - 1],
                device_id=col_peer(k), device_id_type=MESH,
            )
            copy.start()
            out.append(copy)
        started.extend(out)
        return out

    def arrive(copies):
        for copy in copies:
            copy.wait_recv()

    gathering = to_group(0, lambda m: vectors_ref, raw.at[me])
    degree_moves = to_col(0, lambda m: degree_ref, degrees.at[col])
    raw[me] = vectors_ref[...]
    degrees[col] = degree_ref[...]
    arrive(gathering)
    for c in range(n_row):
        whole = jnp.concatenate([raw[c * n_rep + q] for q in range(n_rep)], axis=0)
        turned = whole.astype(F32).T.astype(BF16)
        for q in range(n_rep):
            panels[0, c * n_rep + q] = turned[q * half : (q + 1) * half]

    def products(index):
        panel = panels[index].reshape(n_group * half, count)
        return contract(high_ref[...], panel, ((1,), (0,))) + contract(
            low_ref[...], panel, ((1,), (0,))
        )

    previous = panels[0, me].astype(F32)
    current = previous
    for n in range(DEGREE):
        sends[n] = products(n).astype(BF16).reshape(n_col, half, count)
        moving = to_col(1 + n, lambda m: sends.at[n, m], lands.at[n, col])
        if n == 0:
            arrive(degree_moves)
            sums = degrees[0]
            for s in range(1, n_col):
                sums = sums + degrees[s]
            roots = lax.rsqrt(1.0 + sums)
            padded = jnp.concatenate(
                [roots, jnp.zeros((count - roots.shape[0], roots.shape[1]), F32)], axis=0
            ).T
            for p in range(n_col // 2):
                wide = jnp.broadcast_to(padded[:, p : p + 1], (2 * half, count))
                inv[2 * p] = wide[:half]
                inv[2 * p + 1] = wide[half:]
        lands[n, col] = sends[n, col]
        arrive(moving)
        value = lands[n, 0].astype(F32)
        for s in range(1, n_col):
            value = value + lands[n, s].astype(F32)
        value = value * inv[col]
        if n > 0:
            value = 2.0 * value - previous
        rounded = value.astype(BF16)
        previous, current = current, rounded.astype(F32)
        panels[n + 1, me] = rounded
        if n == DEGREE - 1:
            owners[col] = rounded
            sharing = to_col(DEGREE + 1, lambda m: owners.at[col], owners.at[col])
        gathering = to_group(1 + n, lambda m: panels.at[n + 1, me], panels.at[n + 1, me])
        arrive(gathering)

    images = products(DEGREE) * inv[...].reshape(n_col * half, count)
    block_ref[...] = panels[DEGREE, pl.ds(row * n_rep, n_rep)].reshape(count, count)
    arrive(sharing)
    filtered = owners[...].reshape(n_col * half, count)
    grams[me] = contract(filtered, filtered, ((0,), (0,)))
    gram_moves = to_group(DEGREE + 1, lambda m: grams.at[me], grams.at[me])
    image_high, image_low = split(images)
    cross = contract(filtered, image_high, ((0,), (0,))) + contract(
        filtered, image_low, ((0,), (0,))
    )
    piece = count // n_group
    cross_send[...] = cross.reshape(n_group, piece, count)
    moving = to_group(DEGREE + 2, lambda m: cross_send.at[m], cross_one.at[me])
    cross_one[me] = cross_send[me]
    arrive(moving)
    value = cross_one[0]
    for s in range(1, n_group):
        value = value + cross_one[s]
    cross_two[col] = value
    moving = to_col(DEGREE + 2, lambda m: cross_two.at[col], cross_two.at[col])
    arrive(gram_moves)
    gram = grams[0]
    for s in range(1, n_group):
        gram = gram + grams[s]
    gram_ref[...] = gram
    arrive(moving)
    value = cross_two[0]
    for s in range(1, n_col):
        value = value + cross_two[s]
    cross_all[me] = value
    moving = to_group(DEGREE + 3, lambda m: cross_all.at[me], cross_all.at[me])
    arrive(moving)
    cross_ref[...] = cross_all[...].reshape(count, count)
    for copy in started:
        copy.wait_send()


def finish(n_rep, factor, rep_ref, gram_ref, cross_ref, block_ref, basis_ref, ritz_ref, work, back):
    size = gram_ref.shape[0]
    lines = lax.broadcasted_iota(jnp.int32, (size, size), 0)
    lanes = lax.broadcasted_iota(jnp.int32, (size, size), 1)
    work[...] = gram_ref[...]
    back[...] = (lines == lanes).astype(F32)

    def body(j, carry):
        line = work[pl.ds(j, 1), :]
        other = back[pl.ds(j, 1), :]
        matrix = work[...]
        pivot = jnp.sum(jnp.where(lanes[:1] == j, line, 0.0), axis=1, keepdims=True)
        column = jnp.sum(jnp.where(lanes == j, matrix, 0.0), axis=1, keepdims=True)
        scale = jnp.where(lines[:, :1] > j, column / pivot, 0.0)
        work[...] = matrix - scale * line
        back[...] = back[...] - scale * other
        return carry

    lax.fori_loop(0, size, body, 0)
    diagonal = jnp.sum(jnp.where(lines == lanes, work[...], 0.0), axis=1, keepdims=True)
    back[...] = back[...] * lax.rsqrt(diagonal)
    inverse = back[...]

    def dot(a, b, dims):
        return lax.dot_general(a, b, (dims, ((), ())), precision=HIGHEST, preferred_element_type=F32)

    half = size // n_rep
    own = back[pl.ds(pl.multiple_of(rep_ref[0] * half, half), half), :]
    basis_ref[...] = factor * dot(own, block_ref[...].astype(F32), ((1,), (1,)))
    ritz_ref[...] = factor * dot(dot(inverse, cross_ref[...], ((1,), (0,))), inverse, ((1,), (1,)))


def solution(mesh):
    n_row, n_col, n_rep = (mesh.shape[a] for a in ("row", "col", "rep"))
    n_group = n_row * n_rep
    vmem = pl.BlockSpec(memory_space=pltpu.VMEM)
    smem = pl.BlockSpec(memory_space=pltpu.SMEM)
    shape = jax.ShapeDtypeStruct

    def shards(vectors, tile_values, tile_rows, tile_cols, tile_scales, live_tiles):
        half_vec, local_rows = vectors.shape
        slots, block = tile_values.shape[:2]
        assert local_rows == block and half_vec * n_rep == block
        half = block // n_rep
        count = half_vec * n_rep
        rep = lax.axis_index("rep").astype(jnp.int32).reshape(1)
        chunks = pieces_of(slots, 6)
        lines = -(-(n_col * half // block) // 8) * 8
        high, low, degree = pl.pallas_call(
            functools.partial(assemble, n_col, n_row, chunks),
            out_shape=(
                shape((n_col * half, n_row * block), BF16),
                shape((n_col * half, n_row * block), BF16),
                shape((lines, block), F32),
            ),
            in_specs=[smem] * 5 + [pl.BlockSpec(memory_space=pl.ANY)],
            out_specs=(vmem, vmem, vmem),
            scratch_shapes=[
                pltpu.VMEM((slots, half, block), BF16),
                pltpu.VMEM((n_col * n_row, half, block), F32),
                pltpu.VMEM((n_col, half, block), F32),
                pltpu.SemaphoreType.DMA((chunks,)),
            ],
            name="assemble",
        )(tile_rows, tile_cols, tile_scales, live_tiles, rep, tile_values)
        piece = count // n_group
        gram, cross, filtered = pl.pallas_call(
            functools.partial(exchange, n_row, n_col, n_rep),
            out_shape=(
                shape((count, count), F32), shape((count, count), F32), shape((block, count), BF16),
            ),
            in_specs=[vmem] * 4,
            out_specs=(vmem,) * 3,
            scratch_shapes=[
                pltpu.VMEM((n_group, half_vec, block), BF16),
                pltpu.VMEM((n_col, lines, block), F32),
                pltpu.VMEM((DEGREE + 1, n_group, half, count), BF16),
                pltpu.VMEM((DEGREE, n_col, half, count), BF16),
                pltpu.VMEM((DEGREE, n_col, half, count), BF16),
                pltpu.VMEM((n_col, half, count), BF16),
                pltpu.VMEM((n_col, half, count), F32),
                pltpu.VMEM((n_group, count, count), F32),
                pltpu.VMEM((n_group, piece, count), F32),
                pltpu.VMEM((n_group, piece, count), F32),
                pltpu.VMEM((n_col, piece, count), F32),
                pltpu.VMEM((n_group, piece, count), F32),
                pltpu.SemaphoreType.DMA((DEGREE + 4, n_group - 1)),
                pltpu.SemaphoreType.DMA((DEGREE + 4, n_group - 1)),
                pltpu.SemaphoreType.DMA((DEGREE + 3, n_col - 1)),
                pltpu.SemaphoreType.DMA((DEGREE + 3, n_col - 1)),
            ],
            compiler_params=pltpu.CompilerParams(collective_id=0, has_side_effects=True),
            name="exchange",
        )(high, low, degree, vectors)
        factor = math.sqrt(local_rows * n_row * n_col)
        return pl.pallas_call(
            functools.partial(finish, n_rep, factor),
            out_shape=(shape((half_vec, local_rows), F32), shape((count, count), F32)),
            in_specs=[smem] + [vmem] * 3,
            out_specs=(vmem,) * 2,
            scratch_shapes=[pltpu.VMEM((count, count), F32), pltpu.VMEM((count, count), F32)],
            name="finish",
        )(rep, gram, cross, filtered)

    return jax.shard_map(
        shards,
        mesh=mesh,
        in_specs=(
            P("rep", ("row", "col")),
            P(("row", "col"), None, None),
            P(("row", "col")),
            P(("row", "col")),
            P(("row", "col")),
            P(("row", "col")),
        ),
        out_specs=(P("rep", ("row", "col")), P()),
        check_vma=False,
    )
```

```python
import functools
import math

import jax
import jax.numpy as jnp
from jax import lax
from jax.experimental import pallas as pl
from jax.experimental.pallas import tpu as pltpu
from jax.sharding import PartitionSpec as P

DEGREE = 3
BAND = 16
HIGHEST = lax.Precision.HIGHEST
MESH = pl.DeviceIdType.MESH
F32 = jnp.float32
BF16 = jnp.bfloat16


def pieces_of(count, want):
    while count % want:
        want -= 1
    return want


def assemble(
    row_blocks, panel_blocks, chunks,
    rows_ref, cols_ref, scales_ref, live_ref, rep_ref, tiles_ref,
    high_ref, low_ref, degree_ref, held, total, absolute, sems,
):
    slots, half, block = held.shape
    step = slots // chunks
    copies = []
    first = pl.multiple_of(rep_ref[0] * half, half)
    for c in range(chunks):
        part = pl.ds(c * step, step)
        copy = pltpu.make_async_copy(
            tiles_ref.at[part, pl.ds(first, half), :], held.at[part], sems.at[c]
        )
        copy.start()
        copies.append(copy)
    total[...] = jnp.zeros_like(total)
    absolute[...] = jnp.zeros_like(absolute)
    live = live_ref[0]
    for c in range(chunks):
        copies[c].wait()

        def body(t, carry):
            scale = jnp.where(t < live, scales_ref[t], 0.0)
            row = rows_ref[t]
            values = held[t].astype(F32)
            place = row * panel_blocks + cols_ref[t]
            total[place] = total[place] + values * scale
            absolute[row] = absolute[row] + jnp.abs(values) * scale
            return carry

        lax.fori_loop(c * step, (c + 1) * step, body, 0, unroll=4)
    for r in range(row_blocks):
        for c in range(panel_blocks):
            whole = total[r * panel_blocks + c]
            high = whole.astype(BF16)
            high_ref[r * half : (r + 1) * half, c * block : (c + 1) * block] = high
            low_ref[r * half : (r + 1) * half, c * block : (c + 1) * block] = (
                whole - high.astype(F32)
            ).astype(BF16)
    degree_ref[...] = jnp.zeros_like(degree_ref)
    for p in range(row_blocks // 2):
        pair = absolute[2 * p : 2 * p + 2].reshape(2 * half, block)
        degree_ref[p : p + 1, :] = jnp.sum(pair.T, axis=0, keepdims=True)


def contract(a, b, dims):
    return lax.dot_general(a, b, (dims, ((), ())), preferred_element_type=F32)


def split(value):
    high = value.astype(BF16)
    return high, (value - high.astype(F32)).astype(BF16)


def exact(a, b, dims):
    return lax.dot_general(a, b, (dims, ((), ())), precision=HIGHEST, preferred_element_type=F32)


def eliminate(work, inverse, band):
    size = work.shape[0]
    base = band * BAND
    left = work[base : base + BAND, :size]
    right = work[base : base + BAND, size:]
    places = lax.broadcasted_iota(jnp.int32, (BAND, size), 0)
    columns = [
        jnp.broadcast_to(left[:, base + j : base + j + 1], (BAND, size)) for j in range(BAND)
    ]
    for j in range(BAND):
        root = lax.rsqrt(columns[j][j : j + 1])
        scaled = columns[j] * root
        for k in range(j + 1, BAND):
            columns[k] = columns[k] - scaled * scaled[k : k + 1]
        below = jnp.where(places > j, scaled, 0.0)
        factor = jnp.where(places == j, root, 1.0)
        left = left * factor
        right = right * factor
        left = left - below * left[j : j + 1]
        right = right - below * right[j : j + 1]
    inverse[base : base + BAND, :] = right
    if base + BAND < size:
        rows = jnp.concatenate([left, right], axis=1)
        change = exact(left, rows, ((0,), (0,)))
        work[base + BAND :, :] = work[base + BAND :, :] - change[base + BAND :, :]


def exchange(
    n_row, n_col, n_rep, factor,
    high_ref, low_ref, degree_ref, vectors_ref,
    basis_ref, ritz_ref,
    raw, degrees, panels, sends, lands, owners, inv, grams, cross_send, cross_one, cross_two, cross_all, work, inverse,
    g_send, g_recv, c_send, c_recv,
):
    row, col, rep = lax.axis_index("row"), lax.axis_index("col"), lax.axis_index("rep")
    n_group = n_row * n_rep
    me = row * n_rep + rep
    half = vectors_ref.shape[0]
    count = half * n_rep

    def group_peer(k):
        other = lax.rem(me + k, n_group)
        return (lax.div(other, n_rep), col, lax.rem(other, n_rep))

    def col_peer(k):
        return (row, lax.rem(col + k, n_col), rep)

    barrier = pltpu.get_barrier_semaphore()
    for k in range(1, n_group):
        pl.semaphore_signal(barrier, inc=1, device_id=group_peer(k), device_id_type=MESH)
    for k in range(1, n_col):
        pl.semaphore_signal(barrier, inc=1, device_id=col_peer(k), device_id_type=MESH)
    pl.semaphore_wait(barrier, n_group + n_col - 2)

    started = []

    def to_group(phase, source, target):
        out = []
        for k in range(1, n_group):
            copy = pltpu.make_async_remote_copy(
                src_ref=source(lax.rem(me + k, n_group)), dst_ref=target,
                send_sem=g_send.at[phase, k - 1], recv_sem=g_recv.at[phase, k - 1],
                device_id=group_peer(k), device_id_type=MESH,
            )
            copy.start()
            out.append(copy)
        started.extend(out)
        return out

    def to_col(phase, source, target):
        out = []
        upper = lax.div(2 * col, n_col)
        for s in range(n_col - 1):
            k = (1 - upper) * (n_col - 1 - s) + upper * (1 + s)
            other = lax.rem(col + k, n_col)
            copy = pltpu.make_async_remote_copy(
                src_ref=source(other), dst_ref=target,
                send_sem=c_send.at[phase, k - 1], recv_sem=c_recv.at[phase, k - 1],
                device_id=(row, other, rep), device_id_type=MESH,
            )
            copy.start()
            out.append(copy)
        started.extend(out)
        return out

    def arrive(copies):
        for copy in copies:
            copy.wait_recv()

    gathering = to_group(0, lambda m: vectors_ref, raw.at[me])
    degree_moves = to_col(0, lambda m: degree_ref, degrees.at[col])
    raw[me] = vectors_ref[...]
    degrees[col] = degree_ref[...]
    arrive(gathering)
    for c in range(n_row):
        whole = jnp.concatenate([raw[c * n_rep + q] for q in range(n_rep)], axis=0)
        turned = whole.astype(F32).T.astype(BF16)
        for q in range(n_rep):
            panels[0, c * n_rep + q] = turned[q * half : (q + 1) * half]

    def products(index):
        panel = panels[index].reshape(n_group * half, count)
        return contract(high_ref[...], panel, ((1,), (0,))) + contract(
            low_ref[...], panel, ((1,), (0,))
        )

    previous = panels[0, me].astype(F32)
    current = previous
    for n in range(DEGREE):
        sends[n] = products(n).astype(BF16).reshape(n_col, half, count)
        moving = to_col(1 + n, lambda m: sends.at[n, m], lands.at[n, col])
        if n == 0:
            arrive(degree_moves)
            sums = degrees[0]
            for s in range(1, n_col):
                sums = sums + degrees[s]
            roots = lax.rsqrt(1.0 + sums)
            padded = jnp.concatenate(
                [roots, jnp.zeros((count - roots.shape[0], roots.shape[1]), F32)], axis=0
            ).T
            for p in range(n_col // 2):
                wide = jnp.broadcast_to(padded[:, p : p + 1], (2 * half, count))
                inv[2 * p] = wide[:half]
                inv[2 * p + 1] = wide[half:]
        lands[n, col] = sends[n, col]
        arrive(moving)
        value = lands[n, 0].astype(F32)
        for s in range(1, n_col):
            value = value + lands[n, s].astype(F32)
        value = value * inv[col]
        if n > 0:
            value = 2.0 * value - previous
        rounded = value.astype(BF16)
        previous, current = current, rounded.astype(F32)
        panels[n + 1, me] = rounded
        if n == DEGREE - 1:
            owners[col] = rounded
            sharing = to_col(DEGREE + 1, lambda m: owners.at[col], owners.at[col])
        gathering = to_group(1 + n, lambda m: panels.at[n + 1, me], panels.at[n + 1, me])
        arrive(gathering)

    images = products(DEGREE) * inv[...].reshape(n_col * half, count)
    arrive(sharing)
    filtered = owners[...].reshape(n_col * half, count)
    grams[me] = contract(filtered, filtered, ((0,), (0,)))
    gram_moves = to_group(DEGREE + 1, lambda m: grams.at[me], grams.at[me])
    image_high, image_low = split(images)
    cross = contract(filtered, image_high, ((0,), (0,))) + contract(
        filtered, image_low, ((0,), (0,))
    )
    piece = count // n_group
    cross_send[...] = cross.reshape(n_group, piece, count)
    cross_moves = to_group(DEGREE + 2, lambda m: cross_send.at[m], cross_one.at[me])
    cross_one[me] = cross_send[me]
    arrive(gram_moves)
    gram = grams[0]
    for s in range(1, n_group):
        gram = gram + grams[s]
    work[:, :count] = gram
    work[:, count:] = (
        lax.broadcasted_iota(jnp.int32, (count, count), 0)
        == lax.broadcasted_iota(jnp.int32, (count, count), 1)
    ).astype(F32)
    bands = count // BAND
    eliminate(work, inverse, 0)
    arrive(cross_moves)
    value = cross_one[0]
    for s in range(1, n_group):
        value = value + cross_one[s]
    cross_two[col] = value
    moving = to_col(DEGREE + 2, lambda m: cross_two.at[col], cross_two.at[col])
    for band in range(1, bands - 2):
        eliminate(work, inverse, band)
    arrive(moving)
    value = cross_two[0]
    for s in range(1, n_col):
        value = value + cross_two[s]
    cross_all[me] = value
    moving = to_group(DEGREE + 3, lambda m: cross_all.at[me], cross_all.at[me])
    for band in range(bands - 2, bands):
        eliminate(work, inverse, band)
    block = panels[DEGREE, pl.ds(row * n_rep, n_rep)].reshape(count, count).astype(F32)
    own = inverse[pl.ds(pl.multiple_of(rep * half, half), half), :]
    basis_ref[...] = factor * exact(own, block, ((1,), (1,)))
    whole = inverse[...]
    arrive(moving)
    left = exact(whole, cross_all[...].reshape(count, count), ((1,), (0,)))
    ritz_ref[...] = factor * exact(left, whole, ((1,), (1,)))
    for copy in started:
        copy.wait_send()


def solution(mesh):
    n_row, n_col, n_rep = (mesh.shape[a] for a in ("row", "col", "rep"))
    n_group = n_row * n_rep
    vmem = pl.BlockSpec(memory_space=pltpu.VMEM)
    smem = pl.BlockSpec(memory_space=pltpu.SMEM)
    shape = jax.ShapeDtypeStruct

    def shards(vectors, tile_values, tile_rows, tile_cols, tile_scales, live_tiles):
        half_vec, local_rows = vectors.shape
        slots, block = tile_values.shape[:2]
        assert local_rows == block and half_vec * n_rep == block
        half = block // n_rep
        count = half_vec * n_rep
        rep = lax.axis_index("rep").astype(jnp.int32).reshape(1)
        chunks = pieces_of(slots, 6)
        lines = -(-(n_col * half // block) // 8) * 8
        high, low, degree = pl.pallas_call(
            functools.partial(assemble, n_col, n_row, chunks),
            out_shape=(
                shape((n_col * half, n_row * block), BF16),
                shape((n_col * half, n_row * block), BF16),
                shape((lines, block), F32),
            ),
            in_specs=[smem] * 5 + [pl.BlockSpec(memory_space=pl.ANY)],
            out_specs=(vmem, vmem, vmem),
            scratch_shapes=[
                pltpu.VMEM((slots, half, block), BF16),
                pltpu.VMEM((n_col * n_row, half, block), F32),
                pltpu.VMEM((n_col, half, block), F32),
                pltpu.SemaphoreType.DMA((chunks,)),
            ],
            name="assemble",
        )(tile_rows, tile_cols, tile_scales, live_tiles, rep, tile_values)
        piece = count // n_group
        factor = math.sqrt(local_rows * n_row * n_col)
        return pl.pallas_call(
            functools.partial(exchange, n_row, n_col, n_rep, factor),
            out_shape=(
                shape((half_vec, local_rows), F32), shape((count, count), F32),
            ),
            in_specs=[vmem] * 4,
            out_specs=(vmem,) * 2,
            scratch_shapes=[
                pltpu.VMEM((n_group, half_vec, block), BF16),
                pltpu.VMEM((n_col, lines, block), F32),
                pltpu.VMEM((DEGREE + 1, n_group, half, count), BF16),
                pltpu.VMEM((DEGREE, n_col, half, count), BF16),
                pltpu.VMEM((DEGREE, n_col, half, count), BF16),
                pltpu.VMEM((n_col, half, count), BF16),
                pltpu.VMEM((n_col, half, count), F32),
                pltpu.VMEM((n_group, count, count), F32),
                pltpu.VMEM((n_group, piece, count), F32),
                pltpu.VMEM((n_group, piece, count), F32),
                pltpu.VMEM((n_col, piece, count), F32),
                pltpu.VMEM((n_group, piece, count), F32),
                pltpu.VMEM((count, 2 * count), F32),
                pltpu.VMEM((count, count), F32),
                pltpu.SemaphoreType.DMA((DEGREE + 4, n_group - 1)),
                pltpu.SemaphoreType.DMA((DEGREE + 4, n_group - 1)),
                pltpu.SemaphoreType.DMA((DEGREE + 3, n_col - 1)),
                pltpu.SemaphoreType.DMA((DEGREE + 3, n_col - 1)),
            ],
            compiler_params=pltpu.CompilerParams(collective_id=0, has_side_effects=True),
            name="exchange",
        )(high, low, degree, vectors)

    return jax.shard_map(
        shards,
        mesh=mesh,
        in_specs=(
            P("rep", ("row", "col")),
            P(("row", "col"), None, None),
            P(("row", "col")),
            P(("row", "col")),
            P(("row", "col")),
            P(("row", "col")),
        ),
        out_specs=(P("rep", ("row", "col")), P()),
        check_vma=False,
    )
```

```python
import functools
import math

import jax
import jax.numpy as jnp
from jax import lax
from jax.experimental import pallas as pl
from jax.experimental.pallas import tpu as pltpu
from jax.sharding import PartitionSpec as P

DEGREE = 3
BAND = 16
HIGHEST = lax.Precision.HIGHEST
MESH = pl.DeviceIdType.MESH
F32 = jnp.float32
BF16 = jnp.bfloat16


def pieces_of(count, want):
    while count % want:
        want -= 1
    return want


def assemble(
    row_blocks, panel_blocks, chunks,
    rows_ref, cols_ref, scales_ref, live_ref, rep_ref, tiles_ref,
    high_ref, low_ref, degree_ref, held, total, absolute, sems,
):
    slots, half, block = held.shape
    step = slots // chunks
    copies = []
    first = pl.multiple_of(rep_ref[0] * half, half)
    for c in range(chunks):
        part = pl.ds(c * step, step)
        copy = pltpu.make_async_copy(
            tiles_ref.at[part, pl.ds(first, half), :], held.at[part], sems.at[c]
        )
        copy.start()
        copies.append(copy)
    total[...] = jnp.zeros_like(total)
    absolute[...] = jnp.zeros_like(absolute)
    live = live_ref[0]
    for c in range(chunks):
        copies[c].wait()

        def body(t, carry):
            scale = jnp.where(t < live, scales_ref[t], 0.0)
            row = rows_ref[t]
            values = held[t].astype(F32)
            place = row * panel_blocks + cols_ref[t]
            total[place] = total[place] + values * scale
            absolute[row] = absolute[row] + jnp.abs(values) * scale
            return carry

        lax.fori_loop(c * step, (c + 1) * step, body, 0, unroll=4)
    for r in range(row_blocks):
        for c in range(panel_blocks):
            whole = total[r * panel_blocks + c]
            high = whole.astype(BF16)
            high_ref[r * half : (r + 1) * half, c * block : (c + 1) * block] = high
            low_ref[r * half : (r + 1) * half, c * block : (c + 1) * block] = (
                whole - high.astype(F32)
            ).astype(BF16)
    degree_ref[...] = jnp.zeros_like(degree_ref)
    for p in range(row_blocks // 2):
        pair = absolute[2 * p : 2 * p + 2].reshape(2 * half, block)
        degree_ref[p : p + 1, :] = jnp.sum(pair.T, axis=0, keepdims=True)


def contract(a, b, dims):
    return lax.dot_general(a, b, (dims, ((), ())), preferred_element_type=F32)


def split(value):
    high = value.astype(BF16)
    return high, (value - high.astype(F32)).astype(BF16)


def exact(a, b, dims):
    return lax.dot_general(a, b, (dims, ((), ())), precision=HIGHEST, preferred_element_type=F32)


def eliminate(work, inverse, band):
    size = work.shape[0]
    base = band * BAND
    left = work[base : base + BAND, :size]
    right = work[base : base + BAND, size:]
    places = lax.broadcasted_iota(jnp.int32, (BAND, size), 0)
    columns = [
        jnp.broadcast_to(left[:, base + j : base + j + 1], (BAND, size)) for j in range(BAND)
    ]
    for j in range(BAND):
        root = lax.rsqrt(columns[j][j : j + 1])
        scaled = columns[j] * root
        for k in range(j + 1, BAND):
            columns[k] = columns[k] - scaled * scaled[k : k + 1]
        below = jnp.where(places > j, scaled, 0.0)
        factor = jnp.where(places == j, root, 1.0)
        left = left * factor
        right = right * factor
        left = left - below * left[j : j + 1]
        right = right - below * right[j : j + 1]
    inverse[base : base + BAND, :] = right
    if base + BAND < size:
        rows = jnp.concatenate([left, right], axis=1)
        change = exact(left, rows, ((0,), (0,)))
        work[base + BAND :, :] = work[base + BAND :, :] - change[base + BAND :, :]


def exchange(
    n_row, n_col, n_rep,
    high_ref, low_ref, degree_ref, vectors_ref,
    inverse_ref, cross_ref, block_ref,
    raw, degrees, panels, sends, lands, owners, inv, grams, cross_send, cross_one, cross_two, cross_all, work, inverse,
    g_send, g_recv, c_send, c_recv,
):
    row, col, rep = lax.axis_index("row"), lax.axis_index("col"), lax.axis_index("rep")
    n_group = n_row * n_rep
    me = row * n_rep + rep
    half = vectors_ref.shape[0]
    count = half * n_rep

    def group_peer(k):
        other = lax.rem(me + k, n_group)
        return (lax.div(other, n_rep), col, lax.rem(other, n_rep))

    def col_peer(k):
        return (row, lax.rem(col + k, n_col), rep)

    barrier = pltpu.get_barrier_semaphore()
    for k in range(1, n_group):
        pl.semaphore_signal(barrier, inc=1, device_id=group_peer(k), device_id_type=MESH)
    for k in range(1, n_col):
        pl.semaphore_signal(barrier, inc=1, device_id=col_peer(k), device_id_type=MESH)
    pl.semaphore_wait(barrier, n_group + n_col - 2)

    started = []

    def to_group(phase, source, target):
        out = []
        for k in range(1, n_group):
            copy = pltpu.make_async_remote_copy(
                src_ref=source(lax.rem(me + k, n_group)), dst_ref=target,
                send_sem=g_send.at[phase, k - 1], recv_sem=g_recv.at[phase, k - 1],
                device_id=group_peer(k), device_id_type=MESH,
            )
            copy.start()
            out.append(copy)
        started.extend(out)
        return out

    side = n_col // 2
    upper = lax.div(col, side)
    far = [(1 - upper) * (n_col - 1 - s) + upper * s for s in range(n_col - side)]
    near = [upper * side + lax.rem(col + s, side) for s in range(1, side)]

    def to_col(phase, source, target, others):
        out = []
        for other in others:
            k = lax.rem(other - col + n_col, n_col)
            copy = pltpu.make_async_remote_copy(
                src_ref=source(other), dst_ref=target,
                send_sem=c_send.at[phase, k - 1], recv_sem=c_recv.at[phase, k - 1],
                device_id=(row, other, rep), device_id_type=MESH,
            )
            copy.start()
            out.append(copy)
        started.extend(out)
        return out

    def arrive(copies):
        for copy in copies:
            copy.wait_recv()

    gathering = to_group(0, lambda m: vectors_ref, raw.at[me])
    degree_moves = to_col(0, lambda m: degree_ref, degrees.at[col], far + near)
    raw[me] = vectors_ref[...]
    degrees[col] = degree_ref[...]
    arrive(gathering)
    for c in range(n_row):
        whole = jnp.concatenate([raw[c * n_rep + q] for q in range(n_rep)], axis=0)
        turned = whole.astype(F32).T.astype(BF16)
        for q in range(n_rep):
            panels[0, c * n_rep + q] = turned[q * half : (q + 1) * half]

    def products(index):
        panel = panels[index].reshape(n_group * half, count)
        return contract(high_ref[...], panel, ((1,), (0,))) + contract(
            low_ref[...], panel, ((1,), (0,))
        )

    previous = panels[0, me].astype(F32)
    current = previous
    for n in range(DEGREE):
        moving = []
        panel = panels[n].reshape(n_group * half, count)
        for base, others in (((1 - upper) * side, far), (upper * side, near)):
            part = pl.ds(pl.multiple_of(base * half, half), side * half)
            partial = contract(high_ref[part, :], panel, ((1,), (0,))) + contract(
                low_ref[part, :], panel, ((1,), (0,))
            )
            sends[n, pl.ds(base, side)] = partial.astype(BF16).reshape(side, half, count)
            moving += to_col(1 + n, lambda m: sends.at[n, m], lands.at[n, col], others)
        if n == 0:
            arrive(degree_moves)
            sums = degrees[0]
            for s in range(1, n_col):
                sums = sums + degrees[s]
            roots = lax.rsqrt(1.0 + sums)
            padded = jnp.concatenate(
                [roots, jnp.zeros((count - roots.shape[0], roots.shape[1]), F32)], axis=0
            ).T
            for p in range(n_col // 2):
                wide = jnp.broadcast_to(padded[:, p : p + 1], (2 * half, count))
                inv[2 * p] = wide[:half]
                inv[2 * p + 1] = wide[half:]
        lands[n, col] = sends[n, col]
        arrive(moving)
        value = lands[n, 0].astype(F32)
        for s in range(1, n_col):
            value = value + lands[n, s].astype(F32)
        value = value * inv[col]
        if n > 0:
            value = 2.0 * value - previous
        rounded = value.astype(BF16)
        previous, current = current, rounded.astype(F32)
        panels[n + 1, me] = rounded
        if n == DEGREE - 1:
            owners[col] = rounded
            sharing = to_col(DEGREE + 1, lambda m: owners.at[col], owners.at[col], far + near)
        gathering = to_group(1 + n, lambda m: panels.at[n + 1, me], panels.at[n + 1, me])
        arrive(gathering)

    images = products(DEGREE) * inv[...].reshape(n_col * half, count)
    arrive(sharing)
    filtered = owners[...].reshape(n_col * half, count)
    grams[me] = contract(filtered, filtered, ((0,), (0,)))
    gram_moves = to_group(DEGREE + 1, lambda m: grams.at[me], grams.at[me])
    image_high, image_low = split(images)
    cross = contract(filtered, image_high, ((0,), (0,))) + contract(
        filtered, image_low, ((0,), (0,))
    )
    piece = count // n_group
    cross_send[...] = cross.reshape(n_group, piece, count)
    cross_moves = to_group(DEGREE + 2, lambda m: cross_send.at[m], cross_one.at[me])
    cross_one[me] = cross_send[me]
    arrive(gram_moves)
    gram = grams[0]
    for s in range(1, n_group):
        gram = gram + grams[s]
    work[:, :count] = gram
    work[:, count:] = (
        lax.broadcasted_iota(jnp.int32, (count, count), 0)
        == lax.broadcasted_iota(jnp.int32, (count, count), 1)
    ).astype(F32)
    bands = count // BAND
    eliminate(work, inverse, 0)
    arrive(cross_moves)
    value = cross_one[0]
    for s in range(1, n_group):
        value = value + cross_one[s]
    cross_two[col] = value
    moving = to_col(DEGREE + 2, lambda m: cross_two.at[col], cross_two.at[col], far + near)
    for band in range(1, bands - 2):
        eliminate(work, inverse, band)
    arrive(moving)
    value = cross_two[0]
    for s in range(1, n_col):
        value = value + cross_two[s]
    cross_all[me] = value
    moving = to_group(DEGREE + 3, lambda m: cross_all.at[me], cross_all.at[me])
    for band in range(bands - 2, bands):
        eliminate(work, inverse, band)
    block_ref[...] = panels[DEGREE, pl.ds(row * n_rep, n_rep)].reshape(count, count)
    inverse_ref[...] = inverse[...]
    arrive(moving)
    cross_ref[...] = cross_all[...].reshape(count, count)
    for copy in started:
        copy.wait_send()


def finish(n_rep, factor, rep_ref, inverse_ref, cross_ref, block_ref, basis_ref, ritz_ref):
    size = inverse_ref.shape[0]
    half = size // n_rep
    whole = inverse_ref[...]
    left = exact(whole, cross_ref[...], ((1,), (0,)))
    own = inverse_ref[pl.ds(pl.multiple_of(rep_ref[0] * half, half), half), :]
    basis_ref[...] = factor * exact(own, block_ref[...].astype(F32), ((1,), (1,)))
    ritz_ref[...] = factor * exact(left, whole, ((1,), (1,)))


def solution(mesh):
    n_row, n_col, n_rep = (mesh.shape[a] for a in ("row", "col", "rep"))
    n_group = n_row * n_rep
    vmem = pl.BlockSpec(memory_space=pltpu.VMEM)
    smem = pl.BlockSpec(memory_space=pltpu.SMEM)
    shape = jax.ShapeDtypeStruct

    def shards(vectors, tile_values, tile_rows, tile_cols, tile_scales, live_tiles):
        half_vec, local_rows = vectors.shape
        slots, block = tile_values.shape[:2]
        assert local_rows == block and half_vec * n_rep == block
        half = block // n_rep
        count = half_vec * n_rep
        rep = lax.axis_index("rep").astype(jnp.int32).reshape(1)
        chunks = pieces_of(slots, 6)
        lines = -(-(n_col * half // block) // 8) * 8
        high, low, degree = pl.pallas_call(
            functools.partial(assemble, n_col, n_row, chunks),
            out_shape=(
                shape((n_col * half, n_row * block), BF16),
                shape((n_col * half, n_row * block), BF16),
                shape((lines, block), F32),
            ),
            in_specs=[smem] * 5 + [pl.BlockSpec(memory_space=pl.ANY)],
            out_specs=(vmem, vmem, vmem),
            scratch_shapes=[
                pltpu.VMEM((slots, half, block), BF16),
                pltpu.VMEM((n_col * n_row, half, block), F32),
                pltpu.VMEM((n_col, half, block), F32),
                pltpu.SemaphoreType.DMA((chunks,)),
            ],
            name="assemble",
        )(tile_rows, tile_cols, tile_scales, live_tiles, rep, tile_values)
        piece = count // n_group
        factor = math.sqrt(local_rows * n_row * n_col)
        inverse, cross, filtered = pl.pallas_call(
            functools.partial(exchange, n_row, n_col, n_rep),
            out_shape=(
                shape((count, count), F32), shape((count, count), F32), shape((block, count), BF16),
            ),
            in_specs=[vmem] * 4,
            out_specs=(vmem,) * 3,
            scratch_shapes=[
                pltpu.VMEM((n_group, half_vec, block), BF16),
                pltpu.VMEM((n_col, lines, block), F32),
                pltpu.VMEM((DEGREE + 1, n_group, half, count), BF16),
                pltpu.VMEM((DEGREE, n_col, half, count), BF16),
                pltpu.VMEM((DEGREE, n_col, half, count), BF16),
                pltpu.VMEM((n_col, half, count), BF16),
                pltpu.VMEM((n_col, half, count), F32),
                pltpu.VMEM((n_group, count, count), F32),
                pltpu.VMEM((n_group, piece, count), F32),
                pltpu.VMEM((n_group, piece, count), F32),
                pltpu.VMEM((n_col, piece, count), F32),
                pltpu.VMEM((n_group, piece, count), F32),
                pltpu.VMEM((count, 2 * count), F32),
                pltpu.VMEM((count, count), F32),
                pltpu.SemaphoreType.DMA((DEGREE + 4, n_group - 1)),
                pltpu.SemaphoreType.DMA((DEGREE + 4, n_group - 1)),
                pltpu.SemaphoreType.DMA((DEGREE + 3, n_col - 1)),
                pltpu.SemaphoreType.DMA((DEGREE + 3, n_col - 1)),
            ],
            compiler_params=pltpu.CompilerParams(collective_id=0, has_side_effects=True),
            name="exchange",
        )(high, low, degree, vectors)
        return pl.pallas_call(
            functools.partial(finish, n_rep, factor),
            out_shape=(shape((half_vec, local_rows), F32), shape((count, count), F32)),
            in_specs=[smem] + [vmem] * 3,
            out_specs=(vmem,) * 2,
            name="finish",
        )(rep, inverse, cross, filtered)

    return jax.shard_map(
        shards,
        mesh=mesh,
        in_specs=(
            P("rep", ("row", "col")),
            P(("row", "col"), None, None),
            P(("row", "col")),
            P(("row", "col")),
            P(("row", "col")),
            P(("row", "col")),
        ),
        out_specs=(P("rep", ("row", "col")), P()),
        check_vma=False,
    )
```

```python
import functools
import math

import jax
import jax.numpy as jnp
from jax import lax
from jax.experimental import pallas as pl
from jax.experimental.pallas import tpu as pltpu
from jax.sharding import PartitionSpec as P

DEGREE = 3
BAND = 16
HIGHEST = lax.Precision.HIGHEST
MESH = pl.DeviceIdType.MESH
F32 = jnp.float32
BF16 = jnp.bfloat16


def pieces_of(count, want):
    while count % want:
        want -= 1
    return want


def assemble(
    row_blocks, panel_blocks, chunks,
    rows_ref, cols_ref, scales_ref, live_ref, rep_ref, tiles_ref,
    high_ref, low_ref, degree_ref, held, total, absolute, sems,
):
    slots, half, block = held.shape
    step = slots // chunks
    copies = []
    first = pl.multiple_of(rep_ref[0] * half, half)
    for c in range(chunks):
        part = pl.ds(c * step, step)
        copy = pltpu.make_async_copy(
            tiles_ref.at[part, pl.ds(first, half), :], held.at[part], sems.at[c]
        )
        copy.start()
        copies.append(copy)
    total[...] = jnp.zeros_like(total)
    absolute[...] = jnp.zeros_like(absolute)
    live = live_ref[0]
    for c in range(chunks):
        copies[c].wait()

        def body(t, carry):
            scale = jnp.where(t < live, scales_ref[t], 0.0)
            row = rows_ref[t]
            values = held[t].astype(F32)
            place = row * panel_blocks + cols_ref[t]
            total[place] = total[place] + values * scale
            absolute[row] = absolute[row] + jnp.abs(values) * scale
            return carry

        lax.fori_loop(c * step, (c + 1) * step, body, 0, unroll=4)
    for r in range(row_blocks):
        for c in range(panel_blocks):
            whole = total[r * panel_blocks + c]
            high = whole.astype(BF16)
            high_ref[r * half : (r + 1) * half, c * block : (c + 1) * block] = high
            low_ref[r * half : (r + 1) * half, c * block : (c + 1) * block] = (
                whole - high.astype(F32)
            ).astype(BF16)
    degree_ref[...] = jnp.zeros_like(degree_ref)
    for p in range(row_blocks // 2):
        pair = absolute[2 * p : 2 * p + 2].reshape(2 * half, block)
        degree_ref[p : p + 1, :] = jnp.sum(pair.T, axis=0, keepdims=True)


def contract(a, b, dims):
    return lax.dot_general(a, b, (dims, ((), ())), preferred_element_type=F32)


def split(value):
    high = value.astype(BF16)
    return high, (value - high.astype(F32)).astype(BF16)


def exact(a, b, dims):
    return lax.dot_general(a, b, (dims, ((), ())), precision=HIGHEST, preferred_element_type=F32)


def eliminate(work, inverse, band):
    size = work.shape[0]
    base = band * BAND
    left = work[base : base + BAND, :size]
    right = work[base : base + BAND, size:]
    places = lax.broadcasted_iota(jnp.int32, (BAND, size), 0)
    columns = [
        jnp.broadcast_to(left[:, base + j : base + j + 1], (BAND, size)) for j in range(BAND)
    ]
    for j in range(BAND):
        root = lax.rsqrt(columns[j][j : j + 1])
        scaled = columns[j] * root
        for k in range(j + 1, BAND):
            columns[k] = columns[k] - scaled * scaled[k : k + 1]
        below = jnp.where(places > j, scaled, 0.0)
        factor = jnp.where(places == j, root, 1.0)
        left = left * factor
        right = right * factor
        left = left - below * left[j : j + 1]
        right = right - below * right[j : j + 1]
    inverse[base : base + BAND, :] = right
    if base + BAND < size:
        rows = jnp.concatenate([left, right], axis=1)
        change = exact(left, rows, ((0,), (0,)))
        work[base + BAND :, :] = work[base + BAND :, :] - change[base + BAND :, :]


def exchange(
    n_row, n_col, n_rep,
    high_ref, low_ref, degree_ref, vectors_ref,
    inverse_ref, cross_ref, block_ref,
    raw, degrees, panels, sends, lands, owners, inv, grams, cross_send, cross_one, cross_two, cross_all, work, inverse,
    g_send, g_recv, c_send, c_recv,
):
    row, col, rep = lax.axis_index("row"), lax.axis_index("col"), lax.axis_index("rep")
    n_group = n_row * n_rep
    me = row * n_rep + rep
    half = vectors_ref.shape[0]
    count = half * n_rep

    def group_peer(k):
        other = lax.rem(me + k, n_group)
        return (lax.div(other, n_rep), col, lax.rem(other, n_rep))

    def col_peer(k):
        return (row, lax.rem(col + k, n_col), rep)

    barrier = pltpu.get_barrier_semaphore()
    for k in range(1, n_group):
        pl.semaphore_signal(barrier, inc=1, device_id=group_peer(k), device_id_type=MESH)
    for k in range(1, n_col):
        pl.semaphore_signal(barrier, inc=1, device_id=col_peer(k), device_id_type=MESH)
    pl.semaphore_wait(barrier, n_group + n_col - 2)

    started = []

    def to_group(phase, source, target):
        out = []
        for k in range(1, n_group):
            copy = pltpu.make_async_remote_copy(
                src_ref=source(lax.rem(me + k, n_group)), dst_ref=target,
                send_sem=g_send.at[phase, k - 1], recv_sem=g_recv.at[phase, k - 1],
                device_id=group_peer(k), device_id_type=MESH,
            )
            copy.start()
            out.append(copy)
        started.extend(out)
        return out

    def to_col(phase, source, target):
        out = []
        upper = lax.div(2 * col, n_col)
        for s in range(n_col - 1):
            k = (1 - upper) * (n_col - 1 - s) + upper * (1 + s)
            other = lax.rem(col + k, n_col)
            copy = pltpu.make_async_remote_copy(
                src_ref=source(other), dst_ref=target,
                send_sem=c_send.at[phase, k - 1], recv_sem=c_recv.at[phase, k - 1],
                device_id=(row, other, rep), device_id_type=MESH,
            )
            copy.start()
            out.append(copy)
        started.extend(out)
        return out

    def arrive(copies):
        for copy in copies:
            copy.wait_recv()

    gathering = to_group(0, lambda m: vectors_ref, raw.at[me])
    degree_moves = to_col(0, lambda m: degree_ref, degrees.at[col])
    raw[me] = vectors_ref[...]
    degrees[col] = degree_ref[...]
    arrive(gathering)
    for c in range(n_row):
        whole = jnp.concatenate([raw[c * n_rep + q] for q in range(n_rep)], axis=0)
        turned = whole.astype(F32).T.astype(BF16)
        for q in range(n_rep):
            panels[0, c * n_rep + q] = turned[q * half : (q + 1) * half]

    def products(index):
        panel = panels[index].reshape(n_group * half, count)
        return contract(high_ref[...], panel, ((1,), (0,))) + contract(
            low_ref[...], panel, ((1,), (0,))
        )

    previous = panels[0, me].astype(F32)
    current = previous
    for n in range(DEGREE):
        sends[n] = products(n).astype(BF16).reshape(n_col, half, count)
        moving = to_col(1 + n, lambda m: sends.at[n, m], lands.at[n, col])
        if n == 0:
            arrive(degree_moves)
            sums = degrees[0]
            for s in range(1, n_col):
                sums = sums + degrees[s]
            roots = lax.rsqrt(1.0 + sums)
            padded = jnp.concatenate(
                [roots, jnp.zeros((count - roots.shape[0], roots.shape[1]), F32)], axis=0
            ).T
            for p in range(n_col // 2):
                wide = jnp.broadcast_to(padded[:, p : p + 1], (2 * half, count))
                inv[2 * p] = wide[:half]
                inv[2 * p + 1] = wide[half:]
        lands[n, col] = sends[n, col]
        arrive(moving)
        value = lands[n, 0].astype(F32)
        for s in range(1, n_col):
            value = value + lands[n, s].astype(F32)
        value = value * inv[col]
        if n > 0:
            value = 2.0 * value - previous
        rounded = value.astype(BF16)
        previous, current = current, rounded.astype(F32)
        panels[n + 1, me] = rounded
        if n == DEGREE - 1:
            owners[col] = rounded
            sharing = to_col(DEGREE + 1, lambda m: owners.at[col], owners.at[col])
        gathering = to_group(1 + n, lambda m: panels.at[n + 1, me], panels.at[n + 1, me])
        arrive(gathering)

    images = products(DEGREE) * inv[...].reshape(n_col * half, count)
    arrive(sharing)
    filtered = owners[...].reshape(n_col * half, count)
    grams[me] = contract(filtered, filtered, ((0,), (0,)))
    gram_moves = to_group(DEGREE + 1, lambda m: grams.at[me], grams.at[me])
    image_high, image_low = split(images)
    cross = contract(filtered, image_high, ((0,), (0,))) + contract(
        filtered, image_low, ((0,), (0,))
    )
    piece = count // n_group
    cross_send[...] = cross.reshape(n_group, piece, count)
    cross_moves = to_group(DEGREE + 2, lambda m: cross_send.at[m], cross_one.at[me])
    cross_one[me] = cross_send[me]
    arrive(gram_moves)
    gram = grams[0]
    for s in range(1, n_group):
        gram = gram + grams[s]
    work[:, :count] = gram
    work[:, count:] = (
        lax.broadcasted_iota(jnp.int32, (count, count), 0)
        == lax.broadcasted_iota(jnp.int32, (count, count), 1)
    ).astype(F32)
    bands = count // BAND
    eliminate(work, inverse, 0)
    arrive(cross_moves)
    value = cross_one[0]
    for s in range(1, n_group):
        value = value + cross_one[s]
    cross_two[col] = value
    moving = to_col(DEGREE + 2, lambda m: cross_two.at[col], cross_two.at[col])
    for band in range(1, bands - 2):
        eliminate(work, inverse, band)
    arrive(moving)
    value = cross_two[0]
    for s in range(1, n_col):
        value = value + cross_two[s]
    cross_all[me] = value
    moving = to_group(DEGREE + 3, lambda m: cross_all.at[me], cross_all.at[me])
    for band in range(bands - 2, bands):
        eliminate(work, inverse, band)
    block_ref[...] = panels[DEGREE, pl.ds(row * n_rep, n_rep)].reshape(count, count)
    inverse_ref[...] = inverse[...]
    arrive(moving)
    cross_ref[...] = cross_all[...].reshape(count, count)
    for copy in started:
        copy.wait_send()


def finish(n_rep, factor, rep_ref, inverse_ref, cross_ref, block_ref, basis_ref, ritz_ref):
    size = inverse_ref.shape[0]
    half = size // n_rep
    whole = inverse_ref[...]
    left = exact(whole, cross_ref[...], ((1,), (0,)))
    own = inverse_ref[pl.ds(pl.multiple_of(rep_ref[0] * half, half), half), :]
    basis_ref[...] = factor * exact(own, block_ref[...].astype(F32), ((1,), (1,)))
    ritz_ref[...] = factor * exact(left, whole, ((1,), (1,)))


def solution(mesh):
    n_row, n_col, n_rep = (mesh.shape[a] for a in ("row", "col", "rep"))
    n_group = n_row * n_rep
    vmem = pl.BlockSpec(memory_space=pltpu.VMEM)
    smem = pl.BlockSpec(memory_space=pltpu.SMEM)
    shape = jax.ShapeDtypeStruct

    def shards(vectors, tile_values, tile_rows, tile_cols, tile_scales, live_tiles):
        half_vec, local_rows = vectors.shape
        slots, block = tile_values.shape[:2]
        assert local_rows == block and half_vec * n_rep == block
        half = block // n_rep
        count = half_vec * n_rep
        rep = lax.axis_index("rep").astype(jnp.int32).reshape(1)
        chunks = pieces_of(slots, 6)
        lines = -(-(n_col * half // block) // 8) * 8
        high, low, degree = pl.pallas_call(
            functools.partial(assemble, n_col, n_row, chunks),
            out_shape=(
                shape((n_col * half, n_row * block), BF16),
                shape((n_col * half, n_row * block), BF16),
                shape((lines, block), F32),
            ),
            in_specs=[smem] * 5 + [pl.BlockSpec(memory_space=pl.ANY)],
            out_specs=(vmem, vmem, vmem),
            scratch_shapes=[
                pltpu.VMEM((slots, half, block), BF16),
                pltpu.VMEM((n_col * n_row, half, block), F32),
                pltpu.VMEM((n_col, half, block), F32),
                pltpu.SemaphoreType.DMA((chunks,)),
            ],
            name="assemble",
        )(tile_rows, tile_cols, tile_scales, live_tiles, rep, tile_values)
        piece = count // n_group
        factor = math.sqrt(local_rows * n_row * n_col)
        inverse, cross, filtered = pl.pallas_call(
            functools.partial(exchange, n_row, n_col, n_rep),
            out_shape=(
                shape((count, count), F32), shape((count, count), F32), shape((block, count), BF16),
            ),
            in_specs=[vmem] * 4,
            out_specs=(vmem,) * 3,
            scratch_shapes=[
                pltpu.VMEM((n_group, half_vec, block), BF16),
                pltpu.VMEM((n_col, lines, block), F32),
                pltpu.VMEM((DEGREE + 1, n_group, half, count), BF16),
                pltpu.VMEM((DEGREE, n_col, half, count), BF16),
                pltpu.VMEM((DEGREE, n_col, half, count), BF16),
                pltpu.VMEM((n_col, half, count), BF16),
                pltpu.VMEM((n_col, half, count), F32),
                pltpu.VMEM((n_group, count, count), F32),
                pltpu.VMEM((n_group, piece, count), F32),
                pltpu.VMEM((n_group, piece, count), F32),
                pltpu.VMEM((n_col, piece, count), F32),
                pltpu.VMEM((n_group, piece, count), F32),
                pltpu.VMEM((count, 2 * count), F32),
                pltpu.VMEM((count, count), F32),
                pltpu.SemaphoreType.DMA((DEGREE + 4, n_group - 1)),
                pltpu.SemaphoreType.DMA((DEGREE + 4, n_group - 1)),
                pltpu.SemaphoreType.DMA((DEGREE + 3, n_col - 1)),
                pltpu.SemaphoreType.DMA((DEGREE + 3, n_col - 1)),
            ],
            compiler_params=pltpu.CompilerParams(collective_id=0, has_side_effects=True),
            name="exchange",
        )(high, low, degree, vectors)
        return pl.pallas_call(
            functools.partial(finish, n_rep, factor),
            out_shape=(shape((half_vec, local_rows), F32), shape((count, count), F32)),
            in_specs=[smem] + [vmem] * 3,
            out_specs=(vmem,) * 2,
            name="finish",
        )(rep, inverse, cross, filtered)

    return jax.shard_map(
        shards,
        mesh=mesh,
        in_specs=(
            P("rep", ("row", "col")),
            P(("row", "col"), None, None),
            P(("row", "col")),
            P(("row", "col")),
            P(("row", "col")),
            P(("row", "col")),
        ),
        out_specs=(P("rep", ("row", "col")), P()),
        check_vma=False,
    )
```
